32 devices in a mesh: groups: 1, db: 32 (over z, y, x, core).
Axes of the slice: x: 2, y: 2, z: 4, core: 2. Of those that a mesh axis runs over, the one named last changes fastest.
Arguments:
- queries: bfloat16 [512, 128, 1280], P(('groups', 'db')), may hold values from -8 to 8
- query_lengths: int32 [512], P(('groups', 'db')), may hold values from 32 to 128
- database: bfloat16 [32, 128, 1280], P(('groups', 'db')), may hold values from -8 to 8
- db_lengths: int32 [32], P(('groups', 'db')), may hold values from 32 to 128
- hit_lists: int32 [512, 16], P(('groups', 'db')), may hold values from 0 to 31, all different within a row; in each aligned block of 16 rows (0 to 15, 16 to 31, ...) at most 16 rows name the same one
Outputs:
- pair_scores: float32 [512, 16], P(('groups', 'db'))
- best: float32 [32], P(('groups', 'db'))
The draws below stay inside these ranges and needn't reach their ends.
Inputs may be any that keep to these rules, and one draw needn't show every extreme that they name: `hit_lists`: each row names 16 different database proteins, every database protein is named by some row, and among the 16 rows of one device none is named more than 16 times.
All inputs are finite; a program needn't handle non-finite values.
Results may differ from the reference program's by a relative error of at most 0.0003.
Values may be sent and summed in bfloat16 or wider, within the bound.
A program may use at most 128 MiB of HBM per device.

```python
import math
import jax
import jax.numpy as jnp
import numpy as np
from jax import lax

D = 1280
TILE = 128
H = 16
QP = 16
QUERIES = 512
NDB = 32
MOST = 16


def drawn_tiles(key, count, salt):
    own = jax.random.fold_in(key, salt)
    values = jnp.clip(jax.random.normal(own, (count, TILE, D), jnp.float32), -6.0, 6.0)
    return values.astype(jnp.bfloat16)


def draw_queries(key, part):
    return drawn_tiles(key, QUERIES, 11)


def draw_database(key, part):
    return drawn_tiles(key, NDB, 23)


def touch_ends(entries, own_key, least, largest):
    longest = entries.shape.index(max(entries.shape))
    spots = []
    for shift in (0, 1):
        where = [jax.random.randint(jax.random.fold_in(own_key, axis), (), 0, length) for axis, length in enumerate(entries.shape)]
        where[longest] = (where[longest] + shift) % entries.shape[longest]
        spots.append(tuple(where))
    return entries.at[spots[0]].set(least).at[spots[1]].set(largest)


def assign_block(own_key, own, number, rows, amount, top, limit, skew):
    sequence = jax.random.permutation(own_key, amount)
    heavy_load, ordinary = shares(amount, rows * top, limit, skew, True), shares(amount, rows * top, limit, skew, False)
    places = jnp.arange(amount)

    def named(sizes, rotation):
        used = int((sizes > 0).sum())
        fixed = max(1, used // 4)
        moved = fixed + (places - fixed + rotation * (used - fixed)) % max(1, amount - fixed)
        return jnp.zeros((amount,), jnp.int32).at[sequence[jnp.where(places < fixed, places, moved)]].set(jnp.asarray(sizes, jnp.int32))

    sizes = jnp.where(number % 4 == 0, named(heavy_load, number // 4), named(ordinary, number - number // 4 - 1))
    mixed = jax.random.permutation(jax.random.fold_in(own, 3), amount)
    giver, sink = mixed[0:amount // 2 * 2:2], mixed[1:amount // 2 * 2:2]
    room = jnp.minimum(sizes[giver] - 1, limit - sizes[sink]) // 2
    room = jnp.where((giver == sequence[0]) | (sink == sequence[0]) | (sizes[sink] == 0), 0, jnp.maximum(room, 0))
    moved = jax.random.randint(jax.random.fold_in(own, 4), (amount // 2,), 0, 1 << 20) % (room + 1)
    sizes = sizes.at[giver].add(-moved).at[sink].add(moved)
    labels = jnp.searchsorted(jnp.cumsum(sizes), jnp.arange(rows * top), side="right").astype(jnp.int32)
    listing = labels.reshape(top, rows).T
    listing = listing[jax.random.permutation(jax.random.fold_in(own, 1), rows)]
    rotation = jax.random.randint(jax.random.fold_in(own, 2), (rows, 1), 0, top)
    return jnp.take_along_axis(listing, (jnp.arange(top)[None, :] + rotation) % top, axis=1)


def shares(count, total, bound, skew, full):
    weights = [(1 << 20) // math.isqrt(rank ** skew) + 1 for rank in range(1, count + 1)]
    largest = bound if full else min(bound, max(-(-total // count), total * weights[0] // sum(weights)))
    least = 1 if total - largest >= count - 1 else 0
    given, spare = [largest] + [least] * (count - 1), total - largest - least * (count - 1)
    while spare > 0:
        movable = [i for i in range(1, count) if given[i] < largest] or [i for i in range(1, count) if given[i] < bound]
        mass, left = sum([weights[i] for i in movable]), spare
        for i in movable:
            extra = min(bound - given[i], max(1, left * weights[i] // mass), spare)
            given[i] = given[i] + extra
            spare = spare - extra
    return np.array(given)


def setup_inputs(seed: int = 0, part: int = 0) -> dict:
    key_list = jax.random.split(jax.random.key(seed), 6)
    own_keys = jax.random.split(jax.random.fold_in(key_list[5], part), 6)
    queries = draw_queries(jax.random.fold_in(jax.random.fold_in(key_list[5], part), 71), part)
    query_lengths = touch_ends(jax.random.randint(own_keys[1], (QUERIES,), TILE // 4, TILE + 1), jax.random.fold_in(own_keys[1], 1), TILE // 4, TILE).astype(jnp.int32)
    database = draw_database(jax.random.fold_in(jax.random.fold_in(key_list[5], part), 71), part)
    db_lengths = touch_ends(jax.random.randint(own_keys[3], (NDB,), TILE // 4, TILE + 1), jax.random.fold_in(own_keys[3], 1), TILE // 4, TILE).astype(jnp.int32)
    hit_lists_keys = jax.random.split(jax.random.fold_in(own_keys[4], 1), QUERIES // QP)
    hit_lists_turns = jax.random.permutation(jax.random.fold_in(own_keys[4], 3), QUERIES // QP)
    hit_lists = jax.vmap(lambda own, number: assign_block(jax.random.fold_in(own_keys[4], 2), own, number, QP, NDB, H, MOST, 2))(hit_lists_keys, hit_lists_turns).reshape((QUERIES, H))
    return dict(queries=queries, query_lengths=query_lengths, database=database, db_lengths=db_lengths, hit_lists=hit_lists)


def pair_score(query_tile, db_tile, query_len, db_len):
    features = query_tile.shape[1]
    similar = jnp.dot(query_tile, db_tile.T, preferred_element_type=jnp.float32) / jnp.sqrt(jnp.float32(features))
    row_live = jnp.arange(query_tile.shape[0]) < query_len
    col_live = jnp.arange(db_tile.shape[0]) < db_len
    cell_live = row_live[:, None] & col_live[None, :]
    masked = jnp.where(cell_live, similar, -1e+30)
    row_top = lax.optimization_barrier(jnp.max(masked, axis=1, keepdims=True))
    row_exp = jnp.where(cell_live, jnp.exp(masked - row_top), 0.0)
    row_total = lax.optimization_barrier(jnp.sum(row_exp, axis=1, keepdims=True))
    along_rows = row_exp / jnp.where(row_live[:, None], row_total, 1.0)
    col_top = lax.optimization_barrier(jnp.max(masked, axis=0, keepdims=True))
    col_exp = jnp.where(cell_live, jnp.exp(masked - col_top), 0.0)
    col_total = lax.optimization_barrier(jnp.sum(col_exp, axis=0, keepdims=True))
    along_cols = col_exp / jnp.where(col_live[None, :], col_total, 1.0)
    weights = along_rows + along_cols - along_rows * along_cols
    return jnp.sum(weights * jnp.where(cell_live, similar, 0.0)) / jnp.sum(weights)

def reference(queries, query_lengths, database, db_lengths, hit_lists):
    pair_batch = jax.vmap(pair_score, in_axes=(None, 0, None, 0))

    def one_query(query_index):
        targets = hit_lists[query_index]
        return pair_batch(queries[query_index], database[targets], query_lengths[query_index], db_lengths[targets])
    pair_scores = lax.map(one_query, jnp.arange(queries.shape[0]))
    named = hit_lists[:, :, None] == jnp.arange(NDB).astype(jnp.int32)[None, None, :]
    best = lax.optimization_barrier(jnp.max(jnp.where(named, pair_scores[:, :, None], -10000.0), axis=(0, 1)))
    return (pair_scores, best)
```

```python
import functools
import math

import jax
import jax.numpy as jnp
from jax import lax
from jax.experimental import pallas as pl
from jax.experimental.pallas import tpu as pltpu
from jax.sharding import PartitionSpec as P

DEAD = -1e30
R_Z, R_X, R_Y, R_D0, R_D1, R_SC, R_SX, R_SY, R_SD0, R_SD1 = range(10)
S_UP, S_DN, S_X, S_Y, S_D0, S_D1, S_SC, S_SX, S_SY, S_SD0, S_SD1 = range(11)


def pair_sums(dots, row_limit, row_live, col_limit, col_one, scale):
    s = jnp.minimum(jnp.minimum(dots * scale, col_limit), row_limit)
    row_top = jnp.max(s, axis=1, keepdims=True)
    row_exp = jnp.exp2(s - row_top)
    row_inv = jnp.where(row_live, 1.0 / jnp.sum(row_exp, axis=1, keepdims=True), 0.0)
    col_top = jnp.max(s, axis=0, keepdims=True)
    col_exp = jnp.exp2(s - col_top)
    col_inv = col_one / jnp.sum(col_exp, axis=0, keepdims=True)
    a = row_exp * row_inv
    b = col_exp * col_inv
    w = a + b * (1.0 - a)
    return jnp.sum(w * s, axis=0, keepdims=True), jnp.sum(w, axis=0, keepdims=True)


def kernel(
    n, plane, group,
    qlen_ref, hits_ref, len_ref, q_hbm, db_hbm,
    scores_ref, best_ref,
    q, buf, lens, sim, limit, num, den, table, mine, others,
    send, recv, send_len, recv_len, best_send, best_recv, load,
):
    slabs = n // (2 * plane)
    queries, tile, features = q.shape
    scale = 1.0 / (math.sqrt(features) * math.log(2.0))
    half = tile // 2
    me = lax.axis_index("db")
    core = me % 2
    chip = (me // 2) % plane
    z = me // (2 * plane)
    x_chip = chip + 1 - 2 * (chip % 2)
    y_chip = (chip + 2) % 4
    d_chip = 3 - chip

    def at(zz, chip_, core_):
        return (zz * plane + chip_) * 2 + core_

    sib = at(z, chip, 1 - core)
    x_dev, y_dev = at(z, x_chip, core), at(z, y_chip, core)
    up, down = at(z + 1, chip, core), at(z - 1, chip, core)

    own_copy = pltpu.make_async_copy(db_hbm.at[0], buf.at[me], load.at[0])
    own_copy.start()
    len_copy = pltpu.make_async_copy(len_ref, lens.at[me], load.at[1])
    len_copy.start()
    q_copy = pltpu.make_async_copy(q_hbm, q, load.at[2])
    q_copy.start()

    barrier = pltpu.get_barrier_semaphore()

    def signal(dev):
        pl.semaphore_signal(barrier, inc=1, device_id={"db": dev})

    signal(sib)
    if plane > 1:
        signal(x_dev)
        signal(y_dev)

    @pl.when(z < slabs - 1)
    def _():
        signal(up)

    @pl.when(z > 0)
    def _():
        signal(down)

    ends = jnp.where(z > 0, 1, 0) + jnp.where(z < slabs - 1, 1, 0)
    pl.semaphore_wait(barrier, ends + (3 if plane > 1 else 1))

    def copies(index, dev, skind, rkind, zz, part=None):
        if part is None:
            piece = buf.at[index]
        else:
            piece = buf.at[index, pl.ds(part * half, half)]
        out = [pltpu.make_async_remote_copy(
            src_ref=piece, dst_ref=piece,
            send_sem=send.at[skind, zz], recv_sem=recv.at[rkind, zz],
            device_id={"db": dev})]
        if part != 1:
            out.append(pltpu.make_async_remote_copy(
                src_ref=lens.at[index], dst_ref=lens.at[index],
                send_sem=send_len.at[skind, zz], recv_sem=recv_len.at[rkind, zz],
                device_id={"db": dev}))
        return out

    def start(*args):
        for c in copies(*args):
            c.start()

    def got(index, rkind, zz, part=None):
        for c in copies(index, sib, 0, rkind, zz, part):
            c.wait_recv()

    def sent(index, skind, zz, part=None):
        for c in copies(index, sib, skind, 0, zz, part):
            c.wait_send()

    low = jnp.minimum(z, slabs - 1 - z)
    toward = jnp.where(z <= slabs - 1 - z, 1, -1)

    def order(k):
        near = jnp.where(k % 2 == 1, (k + 1) // 2, -(k // 2))
        return z + jnp.where(k <= 2 * low, near, toward * (k - low))

    def launch(k, first=False):
        zz = order(k)
        own = at(zz, chip, core)
        if not first:
            got(own, R_Z, zz)

        @pl.when((zz <= z) & (z < slabs - 1))
        def _():
            start(own, up, S_UP, R_Z, zz)

        @pl.when((zz >= z) & (z > 0))
        def _():
            start(own, down, S_DN, R_Z, zz)

        if plane > 1:
            start(own, x_dev, S_X, R_X, zz)
            start(own, y_dev, S_Y, R_Y, zz)
        start(own, sib, S_SC, R_SC, zz)

    own_copy.wait()
    len_copy.wait()
    launch(0, first=True)

    rows = lax.broadcasted_iota(jnp.int32, (tile, tile), 0)
    lanes = lax.broadcasted_iota(jnp.int32, (tile, tile), 1)
    chunks = queries // group

    def multiply(chunk, panel):
        left = q[pl.ds(chunk * group, group)].reshape(group * tile, features)
        sim[chunk % 2] = lax.dot_general(
            left, panel, (((1,), (1,)), ((), ())), preferred_element_type=jnp.float32)

    for i in range(queries):
        limit[i] = jnp.where(rows < qlen_ref[i], -DEAD, DEAD)

    def reduce(chunk, pair):
        for j in range(2):
            col_live = lanes[0:1] < lens[pair * 2 + j, 0:1]
            col_limit = jnp.where(col_live, -DEAD, DEAD)
            col_one = jnp.where(col_live, 1.0, 0.0)
            for g in range(group):
                i = chunk * group + g
                row_limit = limit[i]
                row_live = rows < qlen_ref[i]
                dots = sim[chunk % 2, g * tile:(g + 1) * tile, j * tile:(j + 1) * tile]
                top, bottom = pair_sums(dots, row_limit, row_live, col_limit, col_one, scale)
                num[j, i:i + 1] = top
                den[j, i:i + 1] = bottom

    d_lane = lax.broadcasted_iota(jnp.int32, table.shape, 1)
    table[...] = jnp.zeros_like(table)
    sim[...] = jnp.zeros_like(sim)
    num[...] = jnp.zeros_like(num)
    den[...] = jnp.ones_like(den)

    def finish(pair):
        reduce(chunks - 1, pair)
        for j in range(2):
            score = jnp.sum(num[j], axis=1, keepdims=True) * math.log(2.0)
            score = score / jnp.sum(den[j], axis=1, keepdims=True)
            table[...] = jnp.where(d_lane == pair * 2 + j, score, table[...])

    def compute(pair, before):
        panel = buf[pl.ds(pair * 2, 2)].reshape(2 * tile, features)
        multiply(0, panel)
        finish(before)
        for chunk in range(chunks - 1):
            multiply(chunk + 1, panel)
            reduce(chunk, pair)

    q_copy.wait()

    def step(t, before):
        k, j = t // plane, t % plane
        zz = order(k)
        own, other = at(zz, chip, core), at(zz, chip, 1 - core)

        @pl.when(j == 0)
        def _():
            got(other, R_SC, zz)

        @pl.when(j == (1 if plane > 1 else 0))
        def _():
            if plane > 1:
                xt, yt = at(zz, x_chip, core), at(zz, y_chip, core)
                got(xt, R_X, zz)
                start(xt, y_dev, S_D0, R_D0, zz, 0)
                start(xt, sib, S_SX, R_SX, zz)
                got(yt, R_Y, zz)
                start(yt, x_dev, S_D1, R_D1, zz, 1)
                start(yt, sib, S_SY, R_SY, zz)

            @pl.when((k + 1 < slabs) & ((k == 0) | (plane == 1)))
            def _():
                launch(k + 1)

            if plane > 1:
                got(at(zz, x_chip, 1 - core), R_SX, zz)

        spot = chip
        if plane > 1:
            @pl.when(j == 2)
            def _():
                got(at(zz, y_chip, 1 - core), R_SY, zz)

            @pl.when(j == 3)
            def _():
                @pl.when(k + 2 < slabs)
                def _():
                    launch(k + 2)

                dt, od = at(zz, d_chip, core), at(zz, d_chip, 1 - core)
                got(dt, R_D0, zz, 0)
                start(dt, sib, S_SD0, R_SD0, zz, 0)
                got(dt, R_D1, zz, 1)
                start(dt, sib, S_SD1, R_SD1, zz, 1)
                got(od, R_SD0, zz, 0)
                got(od, R_SD1, zz, 1)

            spot = jnp.where(j == 0, chip, jnp.where(j == 1, x_chip, jnp.where(j == 2, y_chip, d_chip)))
        pair = zz * plane + spot
        compute(pair, before)
        return pair

    finish(lax.fori_loop(0, slabs * plane, step, me // 2))

    scores = table[...]
    hits = hits_ref[...]
    named = jnp.zeros(scores.shape, jnp.bool_)
    picked = jnp.zeros(hits.shape, jnp.float32)
    h_lane = lax.broadcasted_iota(jnp.int32, hits.shape, 1)
    for h in range(hits.shape[1]):
        same = d_lane == hits[:, h:h + 1]
        named = named | same
        value = jnp.sum(jnp.where(same, scores, 0.0), axis=1, keepdims=True)
        picked = jnp.where(h_lane == h, value, picked)
    scores_ref[...] = picked
    local = jnp.max(jnp.where(named, scores, -10000.0), axis=0, keepdims=True)
    mine[...] = jnp.broadcast_to(local, mine.shape)

    def tell(dev, slot):
        return pltpu.make_async_remote_copy(
            src_ref=mine, dst_ref=others.at[slot], send_sem=best_send.at[dev],
            recv_sem=best_recv.at[slot], device_id={"db": dev})

    @pl.loop(1, n)
    def _(r):
        tell((me + r) % n, me).start()

    @pl.loop(0, slabs)
    def _(k):
        zz = order(k)
        own = at(zz, chip, core)

        @pl.when((zz <= z) & (z < slabs - 1))
        def _():
            sent(own, S_UP, zz)

        @pl.when((zz >= z) & (z > 0))
        def _():
            sent(own, S_DN, zz)

        sent(own, S_SC, zz)
        if plane > 1:
            sent(own, S_X, zz)
            sent(own, S_Y, zz)
            xt, yt, dt = at(zz, x_chip, core), at(zz, y_chip, core), at(zz, d_chip, core)
            sent(xt, S_D0, zz, 0)
            sent(xt, S_SX, zz)
            sent(yt, S_D1, zz, 1)
            sent(yt, S_SY, zz)
            sent(dt, S_SD0, zz, 0)
            sent(dt, S_SD1, zz, 1)

    @pl.loop(1, n)
    def _(r):
        tell((me + r) % n, (me + r) % n).wait()

    best = lax.fori_loop(
        1, n, lambda r, top: jnp.maximum(top, others[(me + r) % n]), mine[...])
    lane = lax.broadcasted_iota(jnp.int32, best.shape, 1)
    best_ref[...] = jnp.broadcast_to(
        jnp.max(jnp.where(lane == me, best, -jnp.inf), axis=1, keepdims=True), best.shape)


L_Z, L_X, L_Y, L_D, L_SC, L_SX, L_SY, L_SD = range(8)
T_UP, T_DN, T_X, T_Y, T_DUP, T_DDN, T_DX, T_DY, T_SC, T_SX, T_SY, T_SD = range(12)
OWN, XN, YN, DN = range(4)
PIECE, HOP, NEAR, STEP, SLACK = 3.5, 1.5, 1.5, 2.1, 0.0


def plan(slabs):
    unit, first = 2 * PIECE, PIECE + HOP
    due = {}
    for h in range(2):
        for j in range(1, slabs):
            due["chain", j, h] = first + unit * (j - 1) + PIECE * h
            due["spread", j, h] = due["chain", j, h] + 0.01
            due["cross", j, h] = first + unit * j + PIECE * (1 + h)
            due["diag", j, h] = first + unit * (j + 1) + PIECE * h
        due["cross", 0, h] = first + PIECE * h - 0.01
        due["diag", 0, h] = first + unit + 0.1
    if slabs > 1:
        due["late", 0, 0] = max(due["spread", slabs - 1, 1], due["cross", 1, 1]) + 0.05
        for h in range(2):
            due["edge", 0, h] = first + unit * slabs + PIECE
    middle = list(range(1, slabs))
    end = middle[1:-1] + middle[:1] + middle[-1:] if slabs > 2 else middle
    across = [(DN, m, e) for m, e in zip(middle, end)]
    steps = [(OWN, 0, 0), (XN, 0, 0), (YN, 0, 0)] + ([(OWN, 1, 1)] if slabs > 1 else []) + [(DN, 0, 0)]
    for k in range(1, slabs):
        if k + 1 < slabs:
            steps.append((OWN, k + 1, k + 1))
        else:
            steps += across[:-2]
        steps += [(XN, k, k), (YN, k, k)]
    steps += across[-2:]

    def needs(place, m, e):
        if place == OWN:
            return [("chain", m, 1)] if m else []
        if place in (XN, YN):
            return [("cross", m, 1)]
        return [("diag", k, h) for k in (m, e) for h in range(2)] + [("edge", 0, h) for h in range(2) if e == 1]

    slots, now, left = [], NEAR, sorted(due, key=lambda event: due[event])
    for step in steps:
        now = max([now] + [due[event] + NEAR for event in needs(*step)])
        count = sum(due[event] <= now + SLACK for event in left)
        slots.append(left[:count])
        left = left[count:]
        now += STEP
    slots[-1] += left
    return steps, slots


def relay_kernel(
    n, group,
    qlen_ref, len_ref, hits_ref, q_hbm, db_hbm,
    scores_ref, best_ref,
    q, buf, lens, sim, limit, num, den, table, named, mine, others,
    send, recv, send_len, recv_len, best_send, best_recv, load,
):
    plane = 4
    slabs = n // (2 * plane)
    steps, slots = plan(slabs)
    queries, tile, features = q.shape
    scale = 1.0 / (math.sqrt(features) * math.log(2.0))
    half = tile // 2
    me = lax.axis_index("db")
    core = me % 2
    chip = (me // 2) % plane
    z = me // (2 * plane)
    x_chip = chip + 1 - 2 * (chip % 2)
    y_chip = (chip + 2) % 4
    d_chip = 3 - chip
    top = slabs - 1
    edge = (z == 0) | (z == top)

    def at(zz, chip_, core_):
        return (zz * plane + chip_) * 2 + core_

    sib = at(z, chip, 1 - core)
    x_dev, y_dev = at(z, x_chip, core), at(z, y_chip, core)
    up, down = at(z + 1, chip, core), at(z - 1, chip, core)

    own_copy = pltpu.make_async_copy(db_hbm.at[0], buf.at[me], load.at[0])
    own_copy.start()
    q_copy = pltpu.make_async_copy(q_hbm, q, load.at[1])
    q_copy.start()
    lens[me] = jnp.full(lens.shape[1:], len_ref[0], jnp.int32)

    barrier = pltpu.get_barrier_semaphore()

    def signal(dev):
        pl.semaphore_signal(barrier, inc=1, device_id={"db": dev})

    signal(sib)
    signal(x_dev)
    signal(y_dev)

    @pl.when(z < top)
    def _():
        signal(up)

    @pl.when(z > 0)
    def _():
        signal(down)

    pl.semaphore_wait(barrier, jnp.where(z > 0, 1, 0) + jnp.where(z < top, 1, 0) + 3)

    def copies(index, dev, skind, rkind, zz, h):
        piece = buf.at[index, pl.ds(h * half, half)]
        out = [pltpu.make_async_remote_copy(
            src_ref=piece, dst_ref=piece,
            send_sem=send.at[skind, zz, h], recv_sem=recv.at[rkind, zz, h],
            device_id={"db": dev})]
        if h == 0:
            out.append(pltpu.make_async_remote_copy(
                src_ref=lens.at[index], dst_ref=lens.at[index],
                send_sem=send_len.at[skind, zz], recv_sem=recv_len.at[rkind, zz],
                device_id={"db": dev}))
        return out

    def start(*args):
        for c in copies(*args):
            c.start()

    def got(index, rkind, zz, h):
        for c in copies(index, sib, 0, rkind, zz, h):
            c.wait_recv()

    def sent(index, skind, zz, h):
        for c in copies(index, sib, skind, 0, zz, h):
            c.wait_send()

    low = jnp.minimum(z, top - z)
    toward = jnp.where(z <= top - z, 1, -1)

    def order(k):
        near = jnp.where(k % 2 == 1, (k + 1) // 2, -(k // 2))
        return z + jnp.where(k <= 2 * low, near, toward * (k - low))

    def goes_up(zz):
        return (zz <= z) & (z < top)

    def goes_down(zz):
        return (zz >= z) & (z > 0)

    def d_goes_up(zz):
        return goes_up(zz) & ((z + 1 != top) | (zz != top - 1))

    def d_goes_down(zz):
        return goes_down(zz) & ((z != 1) | (zz != 1))

    def launch(zz, h):
        own = at(zz, chip, core)

        @pl.when(goes_up(zz))
        def _():
            start(own, up, T_UP, L_Z, zz, h)

        @pl.when(goes_down(zz))
        def _():
            start(own, down, T_DN, L_Z, zz, h)

        start(own, sib, T_SC, L_SC, zz, h)

    def both_ways(j, action):
        @pl.when(z + j <= top)
        def _():
            action(z + j)

        @pl.when(z - j >= 0)
        def _():
            action(z - j)

    def chain(j, h):
        def arrived(zz):
            got(at(zz, chip, core), L_Z, zz, h)
            launch(zz, h)
        both_ways(j, arrived)

    def spread(k, h):
        zz = order(k)
        own = at(zz, chip, core)
        start(own, x_dev, T_X, L_X, zz, h)
        start(own, y_dev, T_Y, L_Y, zz, 1 - h if k == 0 else h)

    def turn(zz, h):
        if h == 0:
            start(at(zz, x_chip, core), y_dev, T_DY, L_D, zz, 0)
        else:
            start(at(zz, y_chip, core), x_dev, T_DX, L_D, zz, 1)

    def cross(k, h):
        zz = order(k)
        xt, yt = at(zz, x_chip, core), at(zz, y_chip, core)
        g = 1 - h if k == 0 else h
        got(xt, L_X, zz, h)
        if k == 0 and h == 0:
            turn(zz, 0)
        start(xt, sib, T_SX, L_SX, zz, h)
        got(yt, L_Y, zz, g)
        if k == 0 and h == 0:
            turn(zz, 1)
        start(yt, sib, T_SY, L_SY, zz, g)

    def d_arrived(zz, h):
        dt = at(zz, d_chip, core)
        got(dt, L_D, zz, h)

        @pl.when(d_goes_up(zz))
        def _():
            start(dt, up, T_DUP, L_D, zz, h)

        @pl.when(d_goes_down(zz))
        def _():
            start(dt, down, T_DDN, L_D, zz, h)

        start(dt, sib, T_SD, L_SD, zz, h)

    def diag(j, h):
        if j == 0:
            d_arrived(z, h)
        elif j == 1:
            @pl.when(~edge)
            def _():
                both_ways(1, lambda zz: d_arrived(zz, h))
        else:
            both_ways(j, lambda zz: d_arrived(zz, h))

    def late(_, __):
        @pl.when(edge)
        def _():
            for h in range(2):
                turn(order(1), h)

    def edge_arrived(_, h):
        @pl.when(edge)
        def _():
            d_arrived(order(1), h)

    actions = {"chain": chain, "spread": spread, "cross": cross, "diag": diag, "late": late, "edge": edge_arrived}

    own_copy.wait()
    for h in range(2):
        launch(z, h)
        spread(0, h)

    rows = lax.broadcasted_iota(jnp.int32, (tile, tile), 0)
    lanes = lax.broadcasted_iota(jnp.int32, (tile, tile), 1)
    chunks = queries // group

    def multiply(chunk, panel):
        left = q[pl.ds(chunk * group, group)].reshape(group * tile, features)
        sim[chunk % 2] = lax.dot_general(
            left, panel, (((1,), (1,)), ((), ())), preferred_element_type=jnp.float32)

    for i in range(queries):
        limit[i] = jnp.where(rows < qlen_ref[i], -DEAD, DEAD)

    def reduce(chunk, pair):
        for j in range(2):
            col_live = lanes[0:1] < lens[pair * 2 + j]
            col_limit = jnp.where(col_live, -DEAD, DEAD)
            col_one = jnp.where(col_live, 1.0, 0.0)
            for g in range(group):
                i = chunk * group + g
                row_limit = limit[i]
                row_live = rows < qlen_ref[i]
                dots = sim[chunk % 2, g * tile:(g + 1) * tile, j * tile:(j + 1) * tile]
                above, below = pair_sums(dots, row_limit, row_live, col_limit, col_one, scale)
                num[j, i:i + 1] = above
                den[j, i:i + 1] = below

    d_lane = lax.broadcasted_iota(jnp.int32, table.shape, 1)
    table[...] = jnp.zeros_like(table)
    sim[...] = jnp.zeros_like(sim)
    num[...] = jnp.zeros_like(num)
    den[...] = jnp.ones_like(den)
    hits = hits_ref[...]
    same = [d_lane == hits[:, h:h + 1] for h in range(hits.shape[1])]
    named[...] = jnp.where(functools.reduce(jnp.logical_or, same), 1.0, 0.0)

    def finish(pair):
        reduce(chunks - 1, pair)
        for j in range(2):
            d = pair * 2 + j
            score = jnp.sum(num[j], axis=1, keepdims=True) * math.log(2.0)
            score = score / jnp.sum(den[j], axis=1, keepdims=True)
            here = d_lane == d
            table[...] = jnp.where(here, score, table[...])
            counted = jnp.where(here & (named[...] > 0.0), score, -10000.0)
            local = jnp.max(jnp.max(counted, axis=0, keepdims=True), axis=1, keepdims=True)
            mine[d] = jnp.broadcast_to(local, mine.shape[1:])

    def compute(pair, before):
        panel = buf[pl.ds(pair * 2, 2)].reshape(2 * tile, features)
        multiply(0, panel)
        finish(before)
        for chunk in range(chunks - 1):
            multiply(chunk + 1, panel)
            reduce(chunk, pair)

    def tell(d, slot):
        return pltpu.make_async_remote_copy(
            src_ref=mine.at[d], dst_ref=others.at[slot], send_sem=best_send.at[d],
            recv_sem=best_recv.at[slot], device_id={"db": d})

    def tell_pair(pair):
        for j in range(2):
            d = pair * 2 + j

            @pl.when(d != me)
            def _():
                tell(d, me).start()

    def pick(t, values):
        out = jnp.int32(values[0])
        for i in range(1, len(values)):
            if values[i] != values[i - 1]:
                out = jnp.where(t >= i, values[i], out)
        return out

    q_copy.wait()

    def step(t, carry):
        before, done = carry
        for number, events in enumerate(slots):
            if events:
                @pl.when(t == number)
                def _(events=events):
                    for kind, index, h in events:
                        actions[kind](index, h)

        @pl.when(t >= 2)
        def _():
            tell_pair(done)

        place = pick(t, [p for p, _, _ in steps])
        k = jnp.where(edge, pick(t, [e for _, _, e in steps]), pick(t, [m for _, m, _ in steps]))
        zz = order(k)
        for number, (kind, spot) in enumerate(((L_SC, chip), (L_SX, x_chip), (L_SY, y_chip), (L_SD, d_chip))):
            @pl.when(place == number)
            def _(kind=kind, spot=spot):
                for h in range(2):
                    got(at(zz, spot, 1 - core), kind, zz, h)

        spot = jnp.where(place == OWN, chip, jnp.where(place == XN, x_chip, jnp.where(place == YN, y_chip, d_chip)))
        pair = zz * plane + spot
        compute(pair, before)
        return pair, before

    last, done = lax.fori_loop(0, len(steps), step, (me // 2, me // 2))
    tell_pair(done)
    finish(last)
    tell_pair(last)

    scores = table[...]
    picked = jnp.zeros(hits.shape, jnp.float32)
    h_lane = lax.broadcasted_iota(jnp.int32, hits.shape, 1)
    for h in range(hits.shape[1]):
        value = jnp.sum(jnp.where(d_lane == hits[:, h:h + 1], scores, 0.0), axis=1, keepdims=True)
        picked = jnp.where(h_lane == h, value, picked)
    scores_ref[...] = picked

    @pl.loop(0, slabs)
    def _(zz):
        own, dt = at(zz, chip, core), at(zz, d_chip, core)
        xt, yt = at(zz, x_chip, core), at(zz, y_chip, core)
        near_edge = edge & (zz == order(1)) if slabs > 1 else jnp.bool_(False)
        for h in range(2):
            @pl.when(goes_up(zz))
            def _():
                sent(own, T_UP, zz, h)

            @pl.when(goes_down(zz))
            def _():
                sent(own, T_DN, zz, h)

            @pl.when(d_goes_up(zz))
            def _():
                sent(dt, T_DUP, zz, h)

            @pl.when(d_goes_down(zz))
            def _():
                sent(dt, T_DDN, zz, h)

            @pl.when((zz == z) | near_edge)
            def _():
                if h == 0:
                    sent(xt, T_DY, zz, 0)
                else:
                    sent(yt, T_DX, zz, 1)

            sent(own, T_X, zz, h)
            sent(own, T_Y, zz, h)
            sent(own, T_SC, zz, h)
            sent(xt, T_SX, zz, h)
            sent(yt, T_SY, zz, h)
            sent(dt, T_SD, zz, h)

    others[me] = mine[me]

    @pl.loop(1, n)
    def _(r):
        tell((me + r) % n, (me + r) % n).wait()

    best_ref[...] = jnp.broadcast_to(jnp.max(others[...], axis=0), best_ref.shape)


def relay_body(n, queries, query_lengths, database, db_lengths, hit_lists):
    count, tile, features = queries.shape
    slabs = n // 8
    lanes = -(-n // 128) * 128
    group = math.gcd(count, 2)
    vmem = pl.BlockSpec(memory_space=pltpu.VMEM)
    smem = pl.BlockSpec(memory_space=pltpu.SMEM)
    hbm = pl.BlockSpec(memory_space=pl.ANY)
    scores, best = pl.pallas_call(
        functools.partial(relay_kernel, n, group),
        out_shape=(
            jax.ShapeDtypeStruct(hit_lists.shape, jnp.float32),
            jax.ShapeDtypeStruct((8, tile), jnp.float32),
        ),
        in_specs=[smem, smem, vmem, hbm, hbm],
        out_specs=(vmem, vmem),
        scratch_shapes=[
            pltpu.VMEM(queries.shape, queries.dtype),
            pltpu.VMEM((n, tile, features), database.dtype),
            pltpu.VMEM((n, 1, tile), jnp.int32),
            pltpu.VMEM((2, group * tile, 2 * tile), jnp.float32),
            pltpu.VMEM((count, tile, tile), jnp.float32),
            pltpu.VMEM((2, count, tile), jnp.float32),
            pltpu.VMEM((2, count, tile), jnp.float32),
            pltpu.VMEM((count, lanes), jnp.float32),
            pltpu.VMEM((count, lanes), jnp.float32),
            pltpu.VMEM((n, 1, tile), jnp.float32),
            pltpu.VMEM((n, 1, tile), jnp.float32),
            pltpu.SemaphoreType.DMA((12, slabs, 2)),
            pltpu.SemaphoreType.DMA((8, slabs, 2)),
            pltpu.SemaphoreType.DMA((12, slabs)),
            pltpu.SemaphoreType.DMA((8, slabs)),
            pltpu.SemaphoreType.DMA((n,)),
            pltpu.SemaphoreType.DMA((n,)),
            pltpu.SemaphoreType.DMA((2,)),
        ],
        compiler_params=pltpu.CompilerParams(
            collective_id=0, has_side_effects=True, vmem_limit_bytes=60 * 1024 * 1024),
    )(query_lengths, db_lengths, hit_lists, queries, database)
    return scores, best[0, :1]


def body(n, plane, queries, query_lengths, database, db_lengths, hit_lists):
    count, tile, features = queries.shape
    slabs = n // (2 * plane)
    lanes = -(-n // 128) * 128
    group = math.gcd(count, 2)
    length = jnp.broadcast_to(db_lengths[:, None], (8, tile))
    vmem = pl.BlockSpec(memory_space=pltpu.VMEM)
    hbm = pl.BlockSpec(memory_space=pl.ANY)
    scores, best = pl.pallas_call(
        functools.partial(kernel, n, plane, group),
        out_shape=(
            jax.ShapeDtypeStruct(hit_lists.shape, jnp.float32),
            jax.ShapeDtypeStruct((8, lanes), jnp.float32),
        ),
        in_specs=[pl.BlockSpec(memory_space=pltpu.SMEM), vmem, hbm, hbm, hbm],
        out_specs=(vmem, vmem),
        scratch_shapes=[
            pltpu.VMEM(queries.shape, queries.dtype),
            pltpu.VMEM((n, tile, features), database.dtype),
            pltpu.VMEM((n, 8, tile), jnp.int32),
            pltpu.VMEM((2, group * tile, 2 * tile), jnp.float32),
            pltpu.VMEM((count, tile, tile), jnp.float32),
            pltpu.VMEM((2, count, tile), jnp.float32),
            pltpu.VMEM((2, count, tile), jnp.float32),
            pltpu.VMEM((count, lanes), jnp.float32),
            pltpu.VMEM((8, lanes), jnp.float32),
            pltpu.VMEM((n, 8, lanes), jnp.float32),
            pltpu.SemaphoreType.DMA((11, slabs)),
            pltpu.SemaphoreType.DMA((10, slabs)),
            pltpu.SemaphoreType.DMA((11, slabs)),
            pltpu.SemaphoreType.DMA((10, slabs)),
            pltpu.SemaphoreType.DMA((n,)),
            pltpu.SemaphoreType.DMA((n,)),
            pltpu.SemaphoreType.DMA((3,)),
        ],
        compiler_params=pltpu.CompilerParams(
            collective_id=0, has_side_effects=True, vmem_limit_bytes=60 * 1024 * 1024),
    )(query_lengths, hit_lists, length, queries, database)
    return scores, best[0, :1]


def solution(mesh):
    n = mesh.shape["db"]
    plane = 4 if mesh.shape["groups"] == 1 and n % 8 == 0 else 1
    work = functools.partial(relay_body, n) if plane == 4 else functools.partial(body, n, plane)
    return jax.shard_map(
        work,
        mesh=mesh,
        in_specs=(
            P(("groups", "db"), None, None),
            P(("groups", "db")),
            P(("groups", "db"), None, None),
            P(("groups", "db")),
            P(("groups", "db"), None),
        ),
        out_specs=(P(("groups", "db"), None), P(("groups", "db"))),
        check_vma=False,
    )
```

```python
import functools
import math

import jax
import jax.numpy as jnp
from jax import lax
from jax.experimental import pallas as pl
from jax.experimental.pallas import tpu as pltpu
from jax.sharding import PartitionSpec as P

DEAD = -1e30
R_Z, R_X, R_Y, R_D0, R_D1, R_SC, R_SX, R_SY, R_SD0, R_SD1 = range(10)
S_UP, S_DN, S_X, S_Y, S_D0, S_D1, S_SC, S_SX, S_SY, S_SD0, S_SD1 = range(11)


def pair_sums(dots, row_limit, row_live, col_limit, col_one, scale):
    s = jnp.minimum(jnp.minimum(dots * scale, col_limit), row_limit)
    row_top = jnp.max(s, axis=1, keepdims=True)
    row_exp = jnp.exp2(s - row_top)
    row_inv = jnp.where(row_live, 1.0 / jnp.sum(row_exp, axis=1, keepdims=True), 0.0)
    col_top = jnp.max(s, axis=0, keepdims=True)
    col_exp = jnp.exp2(s - col_top)
    col_inv = col_one / jnp.sum(col_exp, axis=0, keepdims=True)
    a = row_exp * row_inv
    b = col_exp * col_inv
    w = a + b * (1.0 - a)
    return jnp.sum(w * s, axis=0, keepdims=True), jnp.sum(w, axis=0, keepdims=True)


def kernel(
    n, plane, group,
    qlen_ref, hits_ref, len_ref, q_hbm, db_hbm,
    scores_ref, best_ref,
    q, buf, lens, sim, limit, num, den, table, mine, others,
    send, recv, send_len, recv_len, best_send, best_recv, load,
):
    slabs = n // (2 * plane)
    queries, tile, features = q.shape
    scale = 1.0 / (math.sqrt(features) * math.log(2.0))
    half = tile // 2
    me = lax.axis_index("db")
    core = me % 2
    chip = (me // 2) % plane
    z = me // (2 * plane)
    x_chip = chip + 1 - 2 * (chip % 2)
    y_chip = (chip + 2) % 4
    d_chip = 3 - chip

    def at(zz, chip_, core_):
        return (zz * plane + chip_) * 2 + core_

    sib = at(z, chip, 1 - core)
    x_dev, y_dev = at(z, x_chip, core), at(z, y_chip, core)
    up, down = at(z + 1, chip, core), at(z - 1, chip, core)

    own_copy = pltpu.make_async_copy(db_hbm.at[0], buf.at[me], load.at[0])
    own_copy.start()
    len_copy = pltpu.make_async_copy(len_ref, lens.at[me], load.at[1])
    len_copy.start()
    q_copy = pltpu.make_async_copy(q_hbm, q, load.at[2])
    q_copy.start()

    barrier = pltpu.get_barrier_semaphore()

    def signal(dev):
        pl.semaphore_signal(barrier, inc=1, device_id={"db": dev})

    signal(sib)
    if plane > 1:
        signal(x_dev)
        signal(y_dev)

    @pl.when(z < slabs - 1)
    def _():
        signal(up)

    @pl.when(z > 0)
    def _():
        signal(down)

    ends = jnp.where(z > 0, 1, 0) + jnp.where(z < slabs - 1, 1, 0)
    pl.semaphore_wait(barrier, ends + (3 if plane > 1 else 1))

    def copies(index, dev, skind, rkind, zz, part=None):
        if part is None:
            piece = buf.at[index]
        else:
            piece = buf.at[index, pl.ds(part * half, half)]
        out = [pltpu.make_async_remote_copy(
            src_ref=piece, dst_ref=piece,
            send_sem=send.at[skind, zz], recv_sem=recv.at[rkind, zz],
            device_id={"db": dev})]
        if part != 1:
            out.append(pltpu.make_async_remote_copy(
                src_ref=lens.at[index], dst_ref=lens.at[index],
                send_sem=send_len.at[skind, zz], recv_sem=recv_len.at[rkind, zz],
                device_id={"db": dev}))
        return out

    def start(*args):
        for c in copies(*args):
            c.start()

    def got(index, rkind, zz, part=None):
        for c in copies(index, sib, 0, rkind, zz, part):
            c.wait_recv()

    def sent(index, skind, zz, part=None):
        for c in copies(index, sib, skind, 0, zz, part):
            c.wait_send()

    low = jnp.minimum(z, slabs - 1 - z)
    toward = jnp.where(z <= slabs - 1 - z, 1, -1)

    def order(k):
        near = jnp.where(k % 2 == 1, (k + 1) // 2, -(k // 2))
        return z + jnp.where(k <= 2 * low, near, toward * (k - low))

    def launch(k, first=False):
        zz = order(k)
        own = at(zz, chip, core)
        if not first:
            got(own, R_Z, zz)

        @pl.when((zz <= z) & (z < slabs - 1))
        def _():
            start(own, up, S_UP, R_Z, zz)

        @pl.when((zz >= z) & (z > 0))
        def _():
            start(own, down, S_DN, R_Z, zz)

        if plane > 1:
            start(own, x_dev, S_X, R_X, zz)
            start(own, y_dev, S_Y, R_Y, zz)
        start(own, sib, S_SC, R_SC, zz)

    own_copy.wait()
    len_copy.wait()
    launch(0, first=True)

    rows = lax.broadcasted_iota(jnp.int32, (tile, tile), 0)
    lanes = lax.broadcasted_iota(jnp.int32, (tile, tile), 1)
    chunks = queries // group

    def multiply(chunk, panel):
        left = q[pl.ds(chunk * group, group)].reshape(group * tile, features)
        sim[chunk % 2] = lax.dot_general(
            left, panel, (((1,), (1,)), ((), ())), preferred_element_type=jnp.float32)

    for i in range(queries):
        limit[i] = jnp.where(rows < qlen_ref[i], -DEAD, DEAD)

    def reduce(chunk, pair):
        for j in range(2):
            col_live = lanes[0:1] < lens[pair * 2 + j, 0:1]
            col_limit = jnp.where(col_live, -DEAD, DEAD)
            col_one = jnp.where(col_live, 1.0, 0.0)
            for g in range(group):
                i = chunk * group + g
                row_limit = limit[i]
                row_live = rows < qlen_ref[i]
                dots = sim[chunk % 2, g * tile:(g + 1) * tile, j * tile:(j + 1) * tile]
                top, bottom = pair_sums(dots, row_limit, row_live, col_limit, col_one, scale)
                num[j, i:i + 1] = top
                den[j, i:i + 1] = bottom

    d_lane = lax.broadcasted_iota(jnp.int32, table.shape, 1)
    table[...] = jnp.zeros_like(table)
    sim[...] = jnp.zeros_like(sim)
    num[...] = jnp.zeros_like(num)
    den[...] = jnp.ones_like(den)

    def finish(pair):
        reduce(chunks - 1, pair)
        for j in range(2):
            score = jnp.sum(num[j], axis=1, keepdims=True) * math.log(2.0)
            score = score / jnp.sum(den[j], axis=1, keepdims=True)
            table[...] = jnp.where(d_lane == pair * 2 + j, score, table[...])

    def compute(pair, before):
        panel = buf[pl.ds(pair * 2, 2)].reshape(2 * tile, features)
        multiply(0, panel)
        finish(before)
        for chunk in range(chunks - 1):
            multiply(chunk + 1, panel)
            reduce(chunk, pair)

    q_copy.wait()

    def step(t, before):
        k, j = t // plane, t % plane
        zz = order(k)
        own, other = at(zz, chip, core), at(zz, chip, 1 - core)

        @pl.when(j == 0)
        def _():
            got(other, R_SC, zz)

        @pl.when(j == (1 if plane > 1 else 0))
        def _():
            if plane > 1:
                xt, yt = at(zz, x_chip, core), at(zz, y_chip, core)
                got(xt, R_X, zz)
                start(xt, y_dev, S_D0, R_D0, zz, 0)
                start(xt, sib, S_SX, R_SX, zz)
                got(yt, R_Y, zz)
                start(yt, x_dev, S_D1, R_D1, zz, 1)
                start(yt, sib, S_SY, R_SY, zz)

            @pl.when((k + 1 < slabs) & ((k == 0) | (plane == 1)))
            def _():
                launch(k + 1)

            if plane > 1:
                got(at(zz, x_chip, 1 - core), R_SX, zz)

        spot = chip
        if plane > 1:
            @pl.when(j == 2)
            def _():
                got(at(zz, y_chip, 1 - core), R_SY, zz)

            @pl.when(j == 3)
            def _():
                @pl.when(k + 2 < slabs)
                def _():
                    launch(k + 2)

                dt, od = at(zz, d_chip, core), at(zz, d_chip, 1 - core)
                got(dt, R_D0, zz, 0)
                start(dt, sib, S_SD0, R_SD0, zz, 0)
                got(dt, R_D1, zz, 1)
                start(dt, sib, S_SD1, R_SD1, zz, 1)
                got(od, R_SD0, zz, 0)
                got(od, R_SD1, zz, 1)

            spot = jnp.where(j == 0, chip, jnp.where(j == 1, x_chip, jnp.where(j == 2, y_chip, d_chip)))
        pair = zz * plane + spot
        compute(pair, before)
        return pair

    finish(lax.fori_loop(0, slabs * plane, step, me // 2))

    scores = table[...]
    hits = hits_ref[...]
    named = jnp.zeros(scores.shape, jnp.bool_)
    picked = jnp.zeros(hits.shape, jnp.float32)
    h_lane = lax.broadcasted_iota(jnp.int32, hits.shape, 1)
    for h in range(hits.shape[1]):
        same = d_lane == hits[:, h:h + 1]
        named = named | same
        value = jnp.sum(jnp.where(same, scores, 0.0), axis=1, keepdims=True)
        picked = jnp.where(h_lane == h, value, picked)
    scores_ref[...] = picked
    local = jnp.max(jnp.where(named, scores, -10000.0), axis=0, keepdims=True)
    mine[...] = jnp.broadcast_to(local, mine.shape)

    def tell(dev, slot):
        return pltpu.make_async_remote_copy(
            src_ref=mine, dst_ref=others.at[slot], send_sem=best_send.at[dev],
            recv_sem=best_recv.at[slot], device_id={"db": dev})

    @pl.loop(1, n)
    def _(r):
        tell((me + r) % n, me).start()

    @pl.loop(0, slabs)
    def _(k):
        zz = order(k)
        own = at(zz, chip, core)

        @pl.when((zz <= z) & (z < slabs - 1))
        def _():
            sent(own, S_UP, zz)

        @pl.when((zz >= z) & (z > 0))
        def _():
            sent(own, S_DN, zz)

        sent(own, S_SC, zz)
        if plane > 1:
            sent(own, S_X, zz)
            sent(own, S_Y, zz)
            xt, yt, dt = at(zz, x_chip, core), at(zz, y_chip, core), at(zz, d_chip, core)
            sent(xt, S_D0, zz, 0)
            sent(xt, S_SX, zz)
            sent(yt, S_D1, zz, 1)
            sent(yt, S_SY, zz)
            sent(dt, S_SD0, zz, 0)
            sent(dt, S_SD1, zz, 1)

    @pl.loop(1, n)
    def _(r):
        tell((me + r) % n, (me + r) % n).wait()

    best = lax.fori_loop(
        1, n, lambda r, top: jnp.maximum(top, others[(me + r) % n]), mine[...])
    lane = lax.broadcasted_iota(jnp.int32, best.shape, 1)
    best_ref[...] = jnp.broadcast_to(
        jnp.max(jnp.where(lane == me, best, -jnp.inf), axis=1, keepdims=True), best.shape)


L_Z, L_X, L_Y, L_D, L_SC, L_SX, L_SY, L_SD = range(8)
T_UP, T_DN, T_X, T_Y, T_DUP, T_DDN, T_DX, T_DY, T_SC, T_SX, T_SY, T_SD = range(12)
OWN, XN, YN, DN = range(4)
LEAST = 32
PIECE, HOP, NEAR, STEP, SLACK = 3.5, 1.5, 1.5, 2.1, 2.2


def capped_sums(dots, row_limit, row_cap, col_limit, col_one, scale):
    s = jnp.minimum(dots * scale, col_limit)
    s = jnp.concatenate([s[:LEAST], jnp.minimum(s[LEAST:], row_limit[LEAST:])], axis=0)
    row_exp = jnp.exp2(s - jnp.max(s, axis=1, keepdims=True))
    row_inv = jnp.broadcast_to(1.0 / jnp.sum(row_exp, axis=1, keepdims=True), dots.shape)
    row_inv = jnp.concatenate([row_inv[:LEAST], jnp.minimum(row_inv[LEAST:], row_cap[LEAST:])], axis=0)
    col_top = jnp.max(s, axis=0, keepdims=True)
    col_exp = jnp.exp2(s - col_top)
    col_inv = col_one / jnp.sum(col_exp, axis=0, keepdims=True)
    a = row_exp * row_inv
    b = col_exp * col_inv
    w = a + b * (1.0 - a)
    return jnp.sum(w * s, axis=0, keepdims=True), jnp.sum(w, axis=0, keepdims=True)


def plan(slabs):
    unit, first = 2 * PIECE, PIECE + HOP
    due = {}
    for h in range(2):
        for j in range(1, slabs):
            due["chain", j, h] = first + unit * (j - 1) + PIECE * h
            due["spread", j, h] = due["chain", j, h] + 0.01
            due["cross", j, h] = first + unit * j + PIECE * (1 + h)
            due["diag", j, h] = first + unit * (j + 1) + PIECE * h
        due["cross", 0, h] = first + PIECE * h - 0.01
        due["diag", 0, h] = first + unit + 0.1
    if slabs > 1:
        due["late", 0, 0] = max(due["spread", slabs - 1, 1], due["cross", 1, 1]) + 0.05
        for h in range(2):
            due["edge", 0, h] = first + unit * slabs + PIECE
    middle = list(range(1, slabs))
    end = middle[1:-1] + middle[:1] + middle[-1:] if slabs > 2 else middle
    across = [(DN, m, e) for m, e in zip(middle, end)]
    steps = [(OWN, 0, 0), (XN, 0, 0), (YN, 0, 0)] + ([(OWN, 1, 1)] if slabs > 1 else []) + [(DN, 0, 0)]
    for k in range(1, slabs):
        if k + 1 < slabs:
            steps.append((OWN, k + 1, k + 1))
        else:
            steps += across[:-2]
        steps += [(XN, k, k), (YN, k, k)]
    steps += across[-2:]

    def needs(place, m, e):
        if place == OWN:
            return [("chain", m, 1)] if m else []
        if place in (XN, YN):
            return [("cross", m, 1)]
        return [("diag", k, h) for k in (m, e) for h in range(2)] + [("edge", 0, h) for h in range(2) if e == 1]

    slots, now, left = [], NEAR, sorted(due, key=lambda event: due[event])
    for step in steps:
        now = max([now] + [due[event] + NEAR for event in needs(*step)])
        count = sum(due[event] <= now + SLACK for event in left)
        slots.append(left[:count])
        left = left[count:]
        now += STEP
    slots[-1] += left
    return steps, slots


def relay_kernel(
    n, group,
    qlen_ref, len_ref, hits_ref, q_hbm, db_hbm,
    scores_ref, best_ref,
    q, buf, lens, sim, limit, cap, num, den, table, named, mine, others,
    send, recv, send_len, recv_len, best_send, best_recv, load,
):
    plane = 4
    slabs = n // (2 * plane)
    steps, slots = plan(slabs)
    queries, tile, features = q.shape
    scale = 1.0 / (math.sqrt(features) * math.log(2.0))
    half = tile // 2
    me = lax.axis_index("db")
    core = me % 2
    chip = (me // 2) % plane
    z = me // (2 * plane)
    x_chip = chip + 1 - 2 * (chip % 2)
    y_chip = (chip + 2) % 4
    d_chip = 3 - chip
    top = slabs - 1
    edge = (z == 0) | (z == top)

    def at(zz, chip_, core_):
        return (zz * plane + chip_) * 2 + core_

    sib = at(z, chip, 1 - core)
    x_dev, y_dev = at(z, x_chip, core), at(z, y_chip, core)
    up, down = at(z + 1, chip, core), at(z - 1, chip, core)

    own_copy = pltpu.make_async_copy(db_hbm.at[0], buf.at[me], load.at[0])
    own_copy.start()
    q_copy = pltpu.make_async_copy(q_hbm, q, load.at[1])
    q_copy.start()
    lens[me] = jnp.full(lens.shape[1:], len_ref[0], jnp.int32)

    barrier = pltpu.get_barrier_semaphore()

    def signal(dev):
        pl.semaphore_signal(barrier, inc=1, device_id={"db": dev})

    signal(sib)
    signal(x_dev)
    signal(y_dev)

    @pl.when(z < top)
    def _():
        signal(up)

    @pl.when(z > 0)
    def _():
        signal(down)

    pl.semaphore_wait(barrier, jnp.where(z > 0, 1, 0) + jnp.where(z < top, 1, 0) + 3)

    def copies(index, dev, skind, rkind, zz, h):
        piece = buf.at[index, pl.ds(h * half, half)]
        out = [pltpu.make_async_remote_copy(
            src_ref=piece, dst_ref=piece,
            send_sem=send.at[skind, zz, h], recv_sem=recv.at[rkind, zz, h],
            device_id={"db": dev})]
        if h == 0:
            out.append(pltpu.make_async_remote_copy(
                src_ref=lens.at[index], dst_ref=lens.at[index],
                send_sem=send_len.at[skind, zz], recv_sem=recv_len.at[rkind, zz],
                device_id={"db": dev}))
        return out

    def start(*args):
        for c in copies(*args):
            c.start()

    def got(index, rkind, zz, h):
        for c in copies(index, sib, 0, rkind, zz, h):
            c.wait_recv()

    def sent(index, skind, zz, h):
        for c in copies(index, sib, skind, 0, zz, h):
            c.wait_send()

    low = jnp.minimum(z, top - z)
    toward = jnp.where(z <= top - z, 1, -1)

    def order(k):
        near = jnp.where(k % 2 == 1, (k + 1) // 2, -(k // 2))
        return z + jnp.where(k <= 2 * low, near, toward * (k - low))

    def goes_up(zz):
        return (zz <= z) & (z < top)

    def goes_down(zz):
        return (zz >= z) & (z > 0)

    def d_goes_up(zz):
        return goes_up(zz) & ((z + 1 != top) | (zz != top - 1))

    def d_goes_down(zz):
        return goes_down(zz) & ((z != 1) | (zz != 1))

    def launch(zz, h):
        own = at(zz, chip, core)

        @pl.when(goes_up(zz))
        def _():
            start(own, up, T_UP, L_Z, zz, h)

        @pl.when(goes_down(zz))
        def _():
            start(own, down, T_DN, L_Z, zz, h)

        start(own, sib, T_SC, L_SC, zz, h)

    def both_ways(j, action):
        @pl.when(z + j <= top)
        def _():
            action(z + j)

        @pl.when(z - j >= 0)
        def _():
            action(z - j)

    def chain(j, h):
        def arrived(zz):
            got(at(zz, chip, core), L_Z, zz, h)
            launch(zz, h)
        both_ways(j, arrived)

    def spread(k, h):
        zz = order(k)
        own = at(zz, chip, core)
        start(own, x_dev, T_X, L_X, zz, h)
        start(own, y_dev, T_Y, L_Y, zz, 1 - h if k == 0 else h)

    def turn(zz, h):
        if h == 0:
            start(at(zz, x_chip, core), y_dev, T_DY, L_D, zz, 0)
        else:
            start(at(zz, y_chip, core), x_dev, T_DX, L_D, zz, 1)

    def cross(k, h):
        zz = order(k)
        xt, yt = at(zz, x_chip, core), at(zz, y_chip, core)
        g = 1 - h if k == 0 else h
        got(xt, L_X, zz, h)
        if k == 0 and h == 0:
            turn(zz, 0)
        start(xt, sib, T_SX, L_SX, zz, h)
        got(yt, L_Y, zz, g)
        if k == 0 and h == 0:
            turn(zz, 1)
        start(yt, sib, T_SY, L_SY, zz, g)

    def d_arrived(zz, h):
        dt = at(zz, d_chip, core)
        got(dt, L_D, zz, h)

        @pl.when(d_goes_up(zz))
        def _():
            start(dt, up, T_DUP, L_D, zz, h)

        @pl.when(d_goes_down(zz))
        def _():
            start(dt, down, T_DDN, L_D, zz, h)

        start(dt, sib, T_SD, L_SD, zz, h)

    def diag(j, h):
        if j == 0:
            d_arrived(z, h)
        elif j == 1:
            @pl.when(~edge)
            def _():
                both_ways(1, lambda zz: d_arrived(zz, h))
        else:
            both_ways(j, lambda zz: d_arrived(zz, h))

    def late(_, __):
        @pl.when(edge)
        def _():
            for h in range(2):
                turn(order(1), h)

    def edge_arrived(_, h):
        @pl.when(edge)
        def _():
            d_arrived(order(1), h)

    actions = {"chain": chain, "spread": spread, "cross": cross, "diag": diag, "late": late, "edge": edge_arrived}

    own_copy.wait()
    for h in range(2):
        launch(z, h)
        spread(0, h)

    rows = lax.broadcasted_iota(jnp.int32, (tile, tile), 0)
    lanes = lax.broadcasted_iota(jnp.int32, (tile, tile), 1)
    chunks = queries // group

    def multiply(chunk, panel):
        left = q[pl.ds(chunk * group, group)].reshape(group * tile, features)
        sim[chunk % 2] = lax.dot_general(
            left, panel, (((1,), (1,)), ((), ())), preferred_element_type=jnp.float32)

    for i in range(queries):
        limit[i] = jnp.where(rows < qlen_ref[i], -DEAD, DEAD)
        cap[i] = jnp.where(rows < qlen_ref[i], 1.0, 0.0)

    def reduce(chunk, pair):
        for j in range(2):
            col_live = lanes[0:1] < lens[pair * 2 + j]
            col_limit = jnp.where(col_live, -DEAD, DEAD)
            col_one = jnp.where(col_live, 1.0, 0.0)
            for g in range(group):
                i = chunk * group + g
                dots = sim[chunk % 2, g * tile:(g + 1) * tile, j * tile:(j + 1) * tile]
                above, below = capped_sums(dots, limit[i], cap[i], col_limit, col_one, scale)
                num[j, i:i + 1] = above
                den[j, i:i + 1] = below

    d_lane = lax.broadcasted_iota(jnp.int32, table.shape, 1)
    table[...] = jnp.zeros_like(table)
    sim[...] = jnp.zeros_like(sim)
    num[...] = jnp.zeros_like(num)
    den[...] = jnp.ones_like(den)
    hits = hits_ref[...]
    same = [d_lane == hits[:, h:h + 1] for h in range(hits.shape[1])]
    named[...] = jnp.where(functools.reduce(jnp.logical_or, same), 1.0, 0.0)

    def finish(pair):
        reduce(chunks - 1, pair)
        for j in range(2):
            d = pair * 2 + j
            score = jnp.sum(num[j], axis=1, keepdims=True) * math.log(2.0)
            score = score / jnp.sum(den[j], axis=1, keepdims=True)
            here = d_lane == d
            table[...] = jnp.where(here, score, table[...])
            counted = jnp.where(here & (named[...] > 0.0), score, -10000.0)
            local = jnp.max(jnp.max(counted, axis=0, keepdims=True), axis=1, keepdims=True)
            mine[d] = jnp.broadcast_to(local, mine.shape[1:])

    def compute(pair, before):
        panel = buf[pl.ds(pair * 2, 2)].reshape(2 * tile, features)
        multiply(0, panel)
        finish(before)
        for chunk in range(chunks - 1):
            multiply(chunk + 1, panel)
            reduce(chunk, pair)

    def tell(d, slot):
        return pltpu.make_async_remote_copy(
            src_ref=mine.at[d], dst_ref=others.at[slot], send_sem=best_send.at[d],
            recv_sem=best_recv.at[slot], device_id={"db": d})

    def tell_pair(pair):
        for j in range(2):
            d = pair * 2 + j

            @pl.when(d != me)
            def _():
                tell(d, me).start()

    def pick(t, values):
        out = jnp.int32(values[0])
        for i in range(1, len(values)):
            if values[i] != values[i - 1]:
                out = jnp.where(t >= i, values[i], out)
        return out

    q_copy.wait()

    def step(t, carry):
        before, done = carry
        for number, events in enumerate(slots):
            if events:
                @pl.when(t == number)
                def _(events=events):
                    for kind, index, h in events:
                        actions[kind](index, h)

        @pl.when(t >= 2)
        def _():
            tell_pair(done)

        place = pick(t, [p for p, _, _ in steps])
        k = jnp.where(edge, pick(t, [e for _, _, e in steps]), pick(t, [m for _, m, _ in steps]))
        zz = order(k)
        for number, (kind, spot) in enumerate(((L_SC, chip), (L_SX, x_chip), (L_SY, y_chip), (L_SD, d_chip))):
            @pl.when(place == number)
            def _(kind=kind, spot=spot):
                for h in range(2):
                    got(at(zz, spot, 1 - core), kind, zz, h)

        spot = jnp.where(place == OWN, chip, jnp.where(place == XN, x_chip, jnp.where(place == YN, y_chip, d_chip)))
        pair = zz * plane + spot
        compute(pair, before)
        return pair, before

    last, done = lax.fori_loop(0, len(steps), step, (me // 2, me // 2))
    tell_pair(done)
    finish(last)
    tell_pair(last)

    scores = table[...]
    picked = jnp.zeros(hits.shape, jnp.float32)
    h_lane = lax.broadcasted_iota(jnp.int32, hits.shape, 1)
    for h in range(hits.shape[1]):
        value = jnp.sum(jnp.where(d_lane == hits[:, h:h + 1], scores, 0.0), axis=1, keepdims=True)
        picked = jnp.where(h_lane == h, value, picked)
    scores_ref[...] = picked

    @pl.loop(0, slabs)
    def _(zz):
        own, dt = at(zz, chip, core), at(zz, d_chip, core)
        xt, yt = at(zz, x_chip, core), at(zz, y_chip, core)
        near_edge = edge & (zz == order(1)) if slabs > 1 else jnp.bool_(False)
        for h in range(2):
            @pl.when(goes_up(zz))
            def _():
                sent(own, T_UP, zz, h)

            @pl.when(goes_down(zz))
            def _():
                sent(own, T_DN, zz, h)

            @pl.when(d_goes_up(zz))
            def _():
                sent(dt, T_DUP, zz, h)

            @pl.when(d_goes_down(zz))
            def _():
                sent(dt, T_DDN, zz, h)

            @pl.when((zz == z) | near_edge)
            def _():
                if h == 0:
                    sent(xt, T_DY, zz, 0)
                else:
                    sent(yt, T_DX, zz, 1)

            sent(own, T_X, zz, h)
            sent(own, T_Y, zz, h)
            sent(own, T_SC, zz, h)
            sent(xt, T_SX, zz, h)
            sent(yt, T_SY, zz, h)
            sent(dt, T_SD, zz, h)

    others[me] = mine[me]

    @pl.loop(1, n)
    def _(r):
        tell((me + r) % n, (me + r) % n).wait()

    best_ref[...] = jnp.broadcast_to(jnp.max(others[...], axis=0), best_ref.shape)


def relay_body(n, queries, query_lengths, database, db_lengths, hit_lists):
    count, tile, features = queries.shape
    slabs = n // 8
    lanes = -(-n // 128) * 128
    group = math.gcd(count, 2)
    vmem = pl.BlockSpec(memory_space=pltpu.VMEM)
    smem = pl.BlockSpec(memory_space=pltpu.SMEM)
    hbm = pl.BlockSpec(memory_space=pl.ANY)
    scores, best = pl.pallas_call(
        functools.partial(relay_kernel, n, group),
        out_shape=(
            jax.ShapeDtypeStruct(hit_lists.shape, jnp.float32),
            jax.ShapeDtypeStruct((8, tile), jnp.float32),
        ),
        in_specs=[smem, smem, vmem, hbm, hbm],
        out_specs=(vmem, vmem),
        scratch_shapes=[
            pltpu.VMEM(queries.shape, queries.dtype),
            pltpu.VMEM((n, tile, features), database.dtype),
            pltpu.VMEM((n, 1, tile), jnp.int32),
            pltpu.VMEM((2, group * tile, 2 * tile), jnp.float32),
            pltpu.VMEM((count, tile, tile), jnp.float32),
            pltpu.VMEM((count, tile, tile), jnp.float32),
            pltpu.VMEM((2, count, tile), jnp.float32),
            pltpu.VMEM((2, count, tile), jnp.float32),
            pltpu.VMEM((count, lanes), jnp.float32),
            pltpu.VMEM((count, lanes), jnp.float32),
            pltpu.VMEM((n, 1, tile), jnp.float32),
            pltpu.VMEM((n, 1, tile), jnp.float32),
            pltpu.SemaphoreType.DMA((12, slabs, 2)),
            pltpu.SemaphoreType.DMA((8, slabs, 2)),
            pltpu.SemaphoreType.DMA((12, slabs)),
            pltpu.SemaphoreType.DMA((8, slabs)),
            pltpu.SemaphoreType.DMA((n,)),
            pltpu.SemaphoreType.DMA((n,)),
            pltpu.SemaphoreType.DMA((2,)),
        ],
        compiler_params=pltpu.CompilerParams(
            collective_id=0, has_side_effects=True, vmem_limit_bytes=60 * 1024 * 1024),
    )(query_lengths, db_lengths, hit_lists, queries, database)
    return scores, best[0, :1]


def body(n, plane, queries, query_lengths, database, db_lengths, hit_lists):
    count, tile, features = queries.shape
    slabs = n // (2 * plane)
    lanes = -(-n // 128) * 128
    group = math.gcd(count, 2)
    length = jnp.broadcast_to(db_lengths[:, None], (8, tile))
    vmem = pl.BlockSpec(memory_space=pltpu.VMEM)
    hbm = pl.BlockSpec(memory_space=pl.ANY)
    scores, best = pl.pallas_call(
        functools.partial(kernel, n, plane, group),
        out_shape=(
            jax.ShapeDtypeStruct(hit_lists.shape, jnp.float32),
            jax.ShapeDtypeStruct((8, lanes), jnp.float32),
        ),
        in_specs=[pl.BlockSpec(memory_space=pltpu.SMEM), vmem, hbm, hbm, hbm],
        out_specs=(vmem, vmem),
        scratch_shapes=[
            pltpu.VMEM(queries.shape, queries.dtype),
            pltpu.VMEM((n, tile, features), database.dtype),
            pltpu.VMEM((n, 8, tile), jnp.int32),
            pltpu.VMEM((2, group * tile, 2 * tile), jnp.float32),
            pltpu.VMEM((count, tile, tile), jnp.float32),
            pltpu.VMEM((2, count, tile), jnp.float32),
            pltpu.VMEM((2, count, tile), jnp.float32),
            pltpu.VMEM((count, lanes), jnp.float32),
            pltpu.VMEM((8, lanes), jnp.float32),
            pltpu.VMEM((n, 8, lanes), jnp.float32),
            pltpu.SemaphoreType.DMA((11, slabs)),
            pltpu.SemaphoreType.DMA((10, slabs)),
            pltpu.SemaphoreType.DMA((11, slabs)),
            pltpu.SemaphoreType.DMA((10, slabs)),
            pltpu.SemaphoreType.DMA((n,)),
            pltpu.SemaphoreType.DMA((n,)),
            pltpu.SemaphoreType.DMA((3,)),
        ],
        compiler_params=pltpu.CompilerParams(
            collective_id=0, has_side_effects=True, vmem_limit_bytes=60 * 1024 * 1024),
    )(query_lengths, hit_lists, length, queries, database)
    return scores, best[0, :1]


def solution(mesh):
    n = mesh.shape["db"]
    plane = 4 if mesh.shape["groups"] == 1 and n % 8 == 0 else 1
    work = functools.partial(relay_body, n) if plane == 4 else functools.partial(body, n, plane)
    return jax.shard_map(
        work,
        mesh=mesh,
        in_specs=(
            P(("groups", "db"), None, None),
            P(("groups", "db")),
            P(("groups", "db"), None, None),
            P(("groups", "db")),
            P(("groups", "db"), None),
        ),
        out_specs=(P(("groups", "db"), None), P(("groups", "db"))),
        check_vma=False,
    )
```
